128 devices in a mesh: section: 8 (over y, z_lo), dp: 16 (over x, z_hi, core).
Axes of the slice: x: 4, y: 4, z: 4 (z_hi: 2, z_lo: 2; z = z_hi * 2 + z_lo), core: 2. Of those that a mesh axis runs over, the one named last changes fastest.
Arguments:
- enter_a: bfloat16 [8, 2048, 7168], P('section', 'dp'), may hold values from -6 to 6
- enter_b: bfloat16 [8, 2048, 7168], P('section', 'dp'), may hold values from -6 to 6
- cotan_a: bfloat16 [8, 2048, 7168], P('section', 'dp'), may hold values from -6 to 6
- cotan_b: bfloat16 [8, 2048, 7168], P('section', 'dp'), may hold values from -6 to 6
- saved_a: bfloat16 [2, 8, 2048, 7168], P(None, 'section', 'dp'), may hold values from -6 to 6
- saved_b: bfloat16 [2, 8, 2048, 7168], P(None, 'section', 'dp'), may hold values from -6 to 6
- norm_gain: float32 [8, 7168], P('section'), may hold values from 0.1 to 1.9
- w_down: bfloat16 [8, 7168, 256], P('section', 'dp'), may hold values from -0.0625 to 0.0625
- latent_gain: float32 [8, 256], P('section'), may hold values from 0.1 to 1.9
- w_up: bfloat16 [8, 256, 7168], P('section', None, 'dp'), may hold values from -0.375 to 0.375
Outputs:
- out_a: bfloat16 [8, 2048, 7168], P('section', 'dp')
- out_b: bfloat16 [8, 2048, 7168], P('section', 'dp')
- back_a: bfloat16 [8, 2048, 7168], P('section', 'dp')
- back_b: bfloat16 [8, 2048, 7168], P('section', 'dp')
- grad_norm_gain: float32 [8, 7168], P('section', 'dp')
- grad_down: float32 [8, 7168, 256], P('section', 'dp')
- grad_latent_gain: float32 [8, 256], P('section', 'dp')
- grad_up: float32 [8, 256, 7168], P('section', None, 'dp')
The draws below stay inside these ranges and needn't reach their ends.
All inputs are finite; a program needn't handle non-finite values.
Results may differ from the reference program's by a relative error of at most 0.035.
Values may be sent and summed in bfloat16 or wider, within the bound.
No kernel may reach another device: no remote copies, remote signals or barrier semaphores. Data moves between devices by JAX's collectives and lax.ppermute only.
A program may use at most 192 MiB of HBM per device.

```python
import jax
import jax.numpy as jnp
from jax import lax

D = 7168
R = 256
TOK_DEV = 128
TICKS = 2
LAYERS = 8
TOKENS = 2048
N_SECTION = 8
N_DP = 16


def spiked(entries, stream_key, source, target, shards_of, factor):
    def block_of(axis_at):
        return (jnp.arange(entries.shape[axis_at]) // (entries.shape[axis_at] // shards_of)).reshape((-1,) + (1,) * (entries.ndim - 1 - axis_at))

    near = jax.random.permutation(stream_key, shards_of)[block_of(target)]
    second = (block_of(target) + shards_of // 2) % shards_of
    return jnp.where((block_of(source) == near) | (block_of(source) == second), factor * entries, entries)


def levels(stream_key, dims, shards, low, top_value):
    level, own = 1.0, jax.random.fold_in(stream_key, 6)
    for axis_at, shards_of in shards:
        heights = jnp.exp(jax.random.uniform(jax.random.fold_in(own, axis_at), (shards_of,), jnp.float32, low / len(shards), top_value / len(shards)))
        level = level * jnp.repeat(heights, dims[axis_at] // shards_of).reshape([-1 if axis == axis_at else 1 for axis in range(len(dims))])
    return level


def noise(own_key, dims, deviation, bound, cuts=(), kind=jnp.bfloat16):
    array = deviation * jax.random.normal(own_key, dims, jnp.float32)
    if cuts:
        array = array * levels(own_key, dims, cuts, -0.22, 0.18)
    return jnp.clip(array, -bound, bound).astype(kind)


def gaussian_with(rng, extent, width, reach, shards, heavy, kind=jnp.bfloat16):
    values = width * jax.random.normal(rng, extent, jnp.float32)
    if shards:
        values = values * levels(rng, extent, shards, -0.22, 0.18)
    return jnp.clip(spiked(values, jax.random.fold_in(rng, 3), *heavy), -reach, reach).astype(kind)


def setup_inputs(seed: int = 0) -> dict:
    streams_of = jax.random.split(jax.random.key(seed), 11)
    enter_a = noise(streams_of[0], (LAYERS, TOKENS, D), 1.0, 6.0, ((0, 8), (1, 16)))
    enter_b = noise(streams_of[1], (LAYERS, TOKENS, D), 1.0, 6.0, ((0, 8), (1, 16)))
    cotan_a = noise(streams_of[2], (LAYERS, TOKENS, D), 1.0, 6.0, ((0, 8), (1, 16)))
    cotan_b = noise(streams_of[3], (LAYERS, TOKENS, D), 1.0, 6.0, ((0, 8), (1, 16)))
    saved_a = gaussian_with(streams_of[4], (TICKS, LAYERS, TOKENS, D), 1.0, 6.0, ((1, 8), (2, 16)), (2, 3, 16, 2.0))
    saved_b = gaussian_with(streams_of[5], (TICKS, LAYERS, TOKENS, D), 1.0, 6.0, ((1, 8), (2, 16)), (2, 3, 16, 2.0))
    norm_gain = jnp.clip(1.0 + 0.18 * jax.random.normal(streams_of[6], (LAYERS, D), jnp.float32), 0.1, 1.9)
    w_down = noise(streams_of[7], (LAYERS, D, R), D ** -0.5, 0.0625, ((0, 8), (1, 16)))
    latent_gain = jnp.clip(1.0 + 0.18 * jax.random.normal(streams_of[8], (LAYERS, R), jnp.float32), 0.1, 1.9)
    w_up = noise(streams_of[9], (LAYERS, R, D), R ** -0.5, 0.375, ((0, 8), (2, 16)))
    return dict(enter_a=enter_a, enter_b=enter_b, cotan_a=cotan_a, cotan_b=cotan_b, saved_a=saved_a, saved_b=saved_b, norm_gain=norm_gain, w_down=w_down, latent_gain=latent_gain, w_up=w_up)


def layer(x, norm_gain, w_down, latent_gain, w_up):
    xf = x.astype(jnp.float32)
    normed = (xf * lax.rsqrt(lax.optimization_barrier(jnp.mean(xf * xf, axis=-1, keepdims=True)) + 1e-06) * norm_gain).astype(jnp.bfloat16)
    latent = jnp.dot(normed, w_down, preferred_element_type=jnp.float32)
    scaled = (latent * lax.rsqrt(lax.optimization_barrier(jnp.mean(latent * latent, axis=-1, keepdims=True)) + 1e-06) * latent_gain).astype(jnp.bfloat16)
    return (xf + jnp.dot(scaled, w_up, preferred_element_type=jnp.float32)).astype(jnp.bfloat16)

def layer_grads(x, cotangent, weights):
    _, pull = jax.vjp(layer, x, *weights)
    return pull(cotangent)

def block_grads(x, cotangent, weights):
    blocks_x = x.reshape(N_DP, TOK_DEV, D)
    blocks_c = cotangent.reshape(N_DP, TOK_DEV, D)
    result = jax.vmap(lambda a, c: layer_grads(a, c, weights))(blocks_x, blocks_c)
    back = result[0].reshape(N_DP * TOK_DEV, D)
    grads = tuple((g.astype(jnp.float32) for g in result[1:]))
    return (back, grads)

def rounded(value):
    narrow = lax.optimization_barrier(value.astype(jnp.bfloat16))
    return narrow.astype(jnp.float32)

def reference(enter_a, enter_b, cotan_a, cotan_b, saved_a, saved_b, norm_gain, w_down, latent_gain, w_up):
    sections = N_SECTION

    def weights(level):
        return (norm_gain[level], w_down[level], latent_gain[level], w_up[level])

    def empty_grads():
        return (jnp.zeros((N_DP, D), jnp.float32), jnp.zeros((N_DP, D, R), jnp.float32), jnp.zeros((N_DP, R), jnp.float32), jnp.zeros((N_DP, R, D), jnp.float32))
    accum_a = [empty_grads() for level in range(sections)]
    accum_b = [empty_grads() for level in range(sections)]
    zero_rows = jnp.zeros_like(enter_a[0])
    cur_a = [enter_a[s] for s in range(sections)]
    cur_b = [enter_b[s] for s in range(sections)]
    cur_ga = [cotan_a[s] for s in range(sections)]
    cur_gb = [cotan_b[s] for s in range(sections)]
    for tick in range(TICKS):
        out_a = [layer(cur_a[s], *weights(s)) for s in range(sections)]
        out_b = [layer(cur_b[s], *weights(sections - 1 - s)) for s in range(sections)]
        back_a = []
        back_b = []
        for s in range(sections):
            back, grads = block_grads(saved_a[tick, s], cur_ga[s], weights(s))
            back_a.append(back)
            accum_a[s] = tuple((p + q for p, q in zip(accum_a[s], grads)))
        for s in range(sections):
            level = sections - 1 - s
            back, grads = block_grads(saved_b[tick, s], cur_gb[s], weights(level))
            back_b.append(back)
            accum_b[level] = tuple((p + q for p, q in zip(accum_b[level], grads)))
        if tick < TICKS - 1:
            cur_a = [zero_rows] + out_a[:-1]
            cur_b = out_b[1:] + [zero_rows]
            cur_ga = back_a[1:] + [zero_rows]
            cur_gb = [zero_rows] + back_b[:-1]
    totals = []
    for k in range(4):
        per_layer = [lax.optimization_barrier(jnp.sum(rounded(accum_a[level][k]) + rounded(accum_b[level][k]), axis=0)) for level in range(sections)]
        totals.append(jnp.stack(per_layer))
    return (jnp.stack(out_a), jnp.stack(out_b), jnp.stack(back_a), jnp.stack(back_b), totals[0], totals[1], totals[2], totals[3])
```

```python
import functools

import jax
import jax.numpy as jnp
from jax import lax
from jax.experimental import pallas as pl
from jax.experimental.pallas import tpu as pltpu
from jax.sharding import PartitionSpec as P

EPS = 1e-06
NX, NZ, NC = 4, 2, 2
NDP = NX * NZ * NC
CH = 512
BF = jnp.bfloat16
F32 = jnp.float32


def dp_move(value, fx=0, fz=0, fc=0):
    pairs = []
    for i in range(NDP):
        x, z, c = i // 4, (i // 2) % 2, i % 2
        pairs.append((i, ((x + fx) % NX) * 4 + (z ^ fz) * 2 + (c ^ fc)))
    return lax.ppermute(value, "dp", pairs)


def mirror(value):
    n = lax.axis_size("section")
    return lax.ppermute(value, "section", [(i, n - 1 - i) for i in range(n)])


def relay(value, distance):
    n = lax.axis_size("section")
    pairs = [(i - distance, i) for i in range(n) if 0 <= i - distance < n]
    return lax.ppermute(value, "section", pairs)


def spread(shard):
    other = dp_move(shard, fz=1)
    both = jnp.stack([shard, other])
    right = dp_move(both, fx=1)
    left = dp_move(both, fx=-1)
    far_a = dp_move(right[:, 0], fx=1)
    far_b = dp_move(left[:, 1], fx=-1)
    mine = (both, right, left, far_a, far_b)
    return mine + tuple(dp_move(p, fc=1) for p in mine)


def nt(a, b):
    return lax.dot_general(a, b, (((1,), (1,)), ((), ())), preferred_element_type=F32)


def nn(a, b):
    return lax.dot_general(a, b, (((1,), (0,)), ((), ())), preferred_element_type=F32)


def weight_copies(idx, pieces, wd, wu, sems):
    x, z, c = idx[0], idx[1], idx[2]
    rows = wd.shape[0] // NDP
    down, up = [], []
    n = 0

    def add(src, dst_ref, group, dx, dz, dc):
        nonlocal n
        place = ((x + dx) & 3) * 4 + ((z + dz) & 1) * 2 + ((c + dc) & 1)
        start = pl.multiple_of(place * rows, 64)
        group.append(pltpu.make_async_copy(src, dst_ref.at[pl.ds(start, rows), :], sems.at[n]))
        n += 1

    for dc in range(2):
        both, right, left, far_a, far_b = pieces[5 * dc : 5 * dc + 5]
        for dz in range(2):
            for ref, dx in ((both, 0), (right, 3), (left, 1)):
                add(ref.at[dz, 0], wd, down, dx, dz, dc)
                add(ref.at[dz, 1], wu, up, dx, dz, dc)
            add(far_a.at[dz], wd, down, 2, dz, dc)
            add(far_b.at[dz], wu, up, 2, dz, dc)
    return down, up


def chunks(ref):
    return ref.shape[1] // CH


def ds(k):
    return pl.ds(pl.multiple_of(k * CH, CH), CH)


def norm_scale(x_ref):
    def step(k, acc):
        xf = x_ref[:, ds(k)].astype(F32)
        sq = xf * xf
        part = sq[:, :128]
        for j in range(1, CH // 128):
            part = part + sq[:, 128 * j : 128 * (j + 1)]
        return acc + part

    acc = lax.fori_loop(0, chunks(x_ref), step, jnp.zeros((x_ref.shape[0], 128), F32))
    return lax.rsqrt(jnp.sum(acc, axis=1, keepdims=True) / x_ref.shape[1] + EPS)


def latent_of(x_ref, gain_ref, wd, nrm_ref, scale):
    def step(k, acc):
        xf = x_ref[:, ds(k)].astype(F32)
        normed = (xf * scale * gain_ref[:, ds(k)]).astype(BF)
        if nrm_ref is not None:
            nrm_ref[:, ds(k)] = normed
        return acc + nn(normed, wd[ds(k), :])

    return lax.fori_loop(0, chunks(x_ref), step, jnp.zeros((x_ref.shape[0], wd.shape[1]), F32))


def forward_kernel(idx, *refs):
    pieces = refs[:10]
    x_ref, gain_ref, lgain_ref, out_ref, wd, wu, sems = refs[10:]
    down, up = weight_copies(idx, pieces, wd, wu, sems)
    for cp in down + up:
        cp.start()
    scale = norm_scale(x_ref)
    for cp in down:
        cp.wait()
    latent = latent_of(x_ref, gain_ref, wd, None, scale)
    scale2 = lax.rsqrt(jnp.mean(latent * latent, axis=1, keepdims=True) + EPS)
    scaled = (latent * scale2 * lgain_ref[...]).astype(BF)
    for cp in up:
        cp.wait()

    def step(k, carry):
        y = x_ref[:, ds(k)].astype(F32) + nt(scaled, wu[ds(k), :])
        out_ref[:, ds(k)] = y.astype(BF)
        return carry

    lax.fori_loop(0, chunks(x_ref), step, 0)


def backward_core(x_ref, g_ref, gain_ref, lgain_ref, wd, wu, down, up, nrm_ref, dn_ref, dgain_ref, back_ref):
    scale = norm_scale(x_ref)
    for cp in down:
        cp.wait()
    latent = latent_of(x_ref, gain_ref, wd, nrm_ref, scale)
    scale2 = lax.rsqrt(jnp.mean(latent * latent, axis=1, keepdims=True) + EPS)
    n2 = latent * scale2
    lgain = lgain_ref[...]
    scaled = (n2 * lgain).astype(BF)
    for cp in up:
        cp.wait()

    def step_g(k, acc):
        return acc + nn(g_ref[:, ds(k)], wu[ds(k), :])

    rows = x_ref.shape[0]
    width = x_ref.shape[1]
    dsc = lax.fori_loop(0, chunks(x_ref), step_g, jnp.zeros((rows, wd.shape[1]), F32))
    dq = dsc.astype(BF).astype(F32)
    dlg = jnp.sum(dq * n2, axis=0, keepdims=True)
    dn2 = dq * lgain
    dlat = (scale2 * (dn2 - n2 * jnp.mean(dn2 * n2, axis=1, keepdims=True))).astype(BF)

    def step_n(k, acc):
        dn_bf = nt(dlat, wd[ds(k), :]).astype(BF)
        dn_ref[:, ds(k)] = dn_bf
        n1 = x_ref[:, ds(k)].astype(F32) * scale
        prod = dn_bf.astype(F32) * n1
        dgain_ref[:, ds(k)] = dgain_ref[:, ds(k)] + jnp.sum(prod, axis=0, keepdims=True)
        prod = prod * gain_ref[:, ds(k)]
        part = prod[:, :128]
        for j in range(1, CH // 128):
            part = part + prod[:, 128 * j : 128 * (j + 1)]
        return acc + part

    acc = lax.fori_loop(0, chunks(x_ref), step_n, jnp.zeros((rows, 128), F32))
    coeff = jnp.sum(acc, axis=1, keepdims=True) / width
    lean = scale * scale * coeff

    def step_x(k, carry):
        dx = dn_ref[:, ds(k)].astype(F32) * (gain_ref[:, ds(k)] * scale) - x_ref[:, ds(k)].astype(F32) * lean
        back_ref[:, ds(k)] = (g_ref[:, ds(k)].astype(F32) + dx).astype(BF)
        return carry

    lax.fori_loop(0, chunks(x_ref), step_x, 0)
    return scaled, dlat, dlg


def backward_first_kernel(idx, *refs):
    pieces = refs[:10]
    (x_ref, g_ref, gain_ref, lgain_ref, back_ref, nrm_ref, sc_ref, dlat_ref, dgain_ref, dlg_ref,
     wd, wu, dn_ref, sems) = refs[10:]
    down, up = weight_copies(idx, pieces, wd, wu, sems)
    for cp in down + up:
        cp.start()
    dgain_ref[...] = jnp.zeros(dgain_ref.shape, F32)
    scaled, dlat, dlg = backward_core(
        x_ref, g_ref, gain_ref, lgain_ref, wd, wu, down, up, nrm_ref, dn_ref, dgain_ref, back_ref
    )
    sc_ref[...] = scaled
    dlat_ref[...] = dlat
    dlg_ref[...] = dlg


def backward_last_kernel(idx, *refs):
    pieces = refs[:10]
    (x_ref, g_ref, gain_ref, lgain_ref, nrm0_ref, g0_ref, sc0_ref, dlat0_ref, dgain0_ref, dlg0_ref,
     back_ref, keep_ref, send_ref,
     wd, wu, dn_ref, nrm_ref, dgain_ref, grads, small, sems, out_sems) = refs[10:]
    down, up = weight_copies(idx, pieces, wd, wu, sems)
    for cp in down + up:
        cp.start()
    dgain_ref[...] = dgain0_ref[...]
    scaled, dlat, dlg = backward_core(
        x_ref, g_ref, gain_ref, lgain_ref, wd, wu, down, up, nrm_ref, dn_ref, dgain_ref, back_ref
    )
    rank = wd.shape[1]
    half = rank // 2
    span = x_ref.shape[1] // (NX * NZ)
    dlat_t = jnp.concatenate([dlat0_ref[...], dlat], axis=0).astype(F32).T.astype(BF)
    sc_t = jnp.concatenate([sc0_ref[...], scaled], axis=0).astype(F32).T.astype(BF)

    def step(k, carry):
        n_all = jnp.concatenate([nrm0_ref[:, ds(k)], nrm_ref[:, ds(k)]], axis=0)
        grads[0, :, ds(k)] = nn(dlat_t, n_all).astype(BF)
        g_all = jnp.concatenate([g0_ref[:, ds(k)], g_ref[:, ds(k)]], axis=0)
        grads[1, :, ds(k)] = nn(sc_t, g_all).astype(BF)
        return carry

    lax.fori_loop(0, chunks(x_ref), step, 0)
    small[...] = jnp.zeros(small.shape, BF)
    small[0:1, :] = dgain_ref[...].astype(BF)
    dlg_all = (dlg0_ref[...] + dlg).astype(BF)
    for j in range(NX * NZ):
        small[1:2, j * span : j * span + rank] = dlg_all
    x, z, c = idx[0], idx[1], idx[2]
    copies = []
    for side, out in ((0, keep_ref), (1, send_ref)):
        row = pl.multiple_of(((c + side) & 1) * half, half)
        for dx in range(NX):
            for dz in range(NZ):
                lane = pl.multiple_of((((x + dx) & 3) * 2 + ((z + dz) & 1)) * span, 128)
                for m in range(2):
                    copies.append((
                        grads.at[m, pl.ds(row, half), pl.ds(lane, span)],
                        out.at[dx, dz, pl.ds(m * half, half), :],
                    ))
                copies.append((small.at[:, pl.ds(lane, span)], out.at[dx, dz, pl.ds(rank, 16), :]))
    started = [pltpu.make_async_copy(a, b, out_sems.at[n]) for n, (a, b) in enumerate(copies)]
    for cp in started:
        cp.start()
    for cp in started:
        cp.wait()


SMEM = functools.partial(pl.BlockSpec, memory_space=pltpu.SMEM)
VMEM = functools.partial(pl.BlockSpec, memory_space=pltpu.VMEM)
ANY = functools.partial(pl.BlockSpec, memory_space=pl.ANY)


def weight_scratch(width, rank):
    return [pltpu.VMEM((width, rank), BF), pltpu.VMEM((width, rank), BF)]


def forward(idx, pieces, x, gain, lgain):
    t, width = x.shape
    rank = lgain.shape[1]
    return pl.pallas_call(
        forward_kernel,
        out_shape=jax.ShapeDtypeStruct(x.shape, BF),
        in_specs=[SMEM()] + [ANY()] * 10 + [VMEM()] * 3,
        out_specs=VMEM(),
        scratch_shapes=weight_scratch(width, rank) + [pltpu.SemaphoreType.DMA((32,))],
        compiler_params=pltpu.CompilerParams(vmem_limit_bytes=32 << 20),
        cost_estimate=pl.CostEstimate(flops=4 * t * width * rank, transcendentals=0, bytes_accessed=4 * width * (t + rank)),
        name="forward",
    )(idx, *pieces, x, gain, lgain)


def backward_first(idx, pieces, x, g, gain, lgain):
    t, width = x.shape
    rank = lgain.shape[1]
    act = jax.ShapeDtypeStruct(x.shape, BF)
    lat = jax.ShapeDtypeStruct((t, rank), BF)
    return pl.pallas_call(
        backward_first_kernel,
        out_shape=(act, act, lat, lat, jax.ShapeDtypeStruct((1, width), F32), jax.ShapeDtypeStruct((1, rank), F32)),
        in_specs=[SMEM()] + [ANY()] * 10 + [VMEM()] * 4,
        out_specs=(VMEM(),) * 6,
        scratch_shapes=weight_scratch(width, rank) + [pltpu.VMEM(x.shape, BF), pltpu.SemaphoreType.DMA((32,))],
        compiler_params=pltpu.CompilerParams(vmem_limit_bytes=40 << 20),
        cost_estimate=pl.CostEstimate(flops=6 * t * width * rank, transcendentals=0, bytes_accessed=4 * width * (2 * t + rank)),
        name="backward_first",
    )(idx, *pieces, x, g, gain, lgain)


def backward_last(idx, pieces, x, g, gain, lgain, first, g0):
    t, width = x.shape
    rank = lgain.shape[1]
    act = jax.ShapeDtypeStruct(x.shape, BF)
    span = width // (NX * NZ)
    block = jax.ShapeDtypeStruct((NX, NZ, rank + 16, span), BF)
    _, nrm0, sc0, dlat0, dgain0, dlg0 = first
    return pl.pallas_call(
        backward_last_kernel,
        out_shape=(act, block, block),
        in_specs=[SMEM()] + [ANY()] * 10 + [VMEM()] * 10,
        out_specs=(VMEM(), ANY(), ANY()),
        scratch_shapes=weight_scratch(width, rank)
        + [
            pltpu.VMEM(x.shape, BF),
            pltpu.VMEM(x.shape, BF),
            pltpu.VMEM((1, width), F32),
            pltpu.VMEM((2, rank, width), BF),
            pltpu.VMEM((16, width), BF),
            pltpu.SemaphoreType.DMA((32,)),
            pltpu.SemaphoreType.DMA((NX * NZ * 6,)),
        ],
        compiler_params=pltpu.CompilerParams(vmem_limit_bytes=48 << 20),
        cost_estimate=pl.CostEstimate(flops=14 * t * width * rank, transcendentals=0, bytes_accessed=4 * width * (4 * t + 2 * rank)),
        name="backward_last",
    )(idx, *pieces, x, g, gain, lgain, nrm0, g0, sc0, dlat0, dgain0, dlg0)


def gather_sums(keep, send):
    half = 128
    recv = dp_move(send, fc=1)

    def both(dx):
        return keep[dx].astype(F32) + recv[dx].astype(F32)

    far = both(2).astype(BF)
    got_a = dp_move(far[:, :half], fx=1).astype(F32)
    got_b = dp_move(far[:, half:], fx=-1).astype(F32)
    rows = keep.shape[2]
    got_a = jnp.pad(got_a, ((0, 0), (0, rows - half), (0, 0)))
    got_b = jnp.pad(got_b, ((0, 0), (half, 0), (0, 0)))
    from_left = dp_move((both(1) + got_a).astype(BF), fx=1)
    from_right = dp_move((both(3) + got_b).astype(BF), fx=-1)
    total = both(0) + from_left.astype(F32) + from_right.astype(F32)
    across = dp_move(total[1].astype(BF), fz=1)
    return total[0] + across.astype(F32)


def body(enter_a, enter_b, cotan_a, cotan_b, saved_a, saved_b, norm_gain, w_down, latent_gain, w_up):
    place = lax.axis_index("dp")
    core = place % 2
    idx = jnp.stack([place // 4, (place // 2) % 2, core]).astype(jnp.int32)
    width = norm_gain.shape[1]
    rank = latent_gain.shape[1]
    cols = w_up.shape[2]

    shard = jnp.stack([w_down[0], w_up[0].T])
    gains = jnp.concatenate([norm_gain[0], latent_gain[0]]).reshape(-1, 128)
    own = spread(shard)
    other = spread(mirror(shard))
    gains_m = mirror(gains).reshape(1, -1)
    gain_a, lgain_a = norm_gain, latent_gain
    gain_b, lgain_b = gains_m[:, :width], gains_m[:, width:]

    first_a = backward_first(idx, own, saved_a[0, 0], cotan_a[0], gain_a, lgain_a)
    ga = relay(first_a[0], -1)
    xa = relay(forward(idx, own, enter_a[0], gain_a, lgain_a), 1)
    first_b = backward_first(idx, other, saved_b[0, 0], cotan_b[0], gain_b, lgain_b)
    gb = relay(first_b[0], 1)
    xb = relay(forward(idx, other, enter_b[0], gain_b, lgain_b), -1)

    back_a, keep_a, send_a = backward_last(idx, own, saved_a[1, 0], ga, gain_a, lgain_a, first_a, cotan_a[0])
    back_b, keep_b, send_b = backward_last(idx, other, saved_b[1, 0], gb, gain_b, lgain_b, first_b, cotan_b[0])
    sum_b = gather_sums(keep_b, send_b)
    sum_a = gather_sums(keep_a, send_a)
    total = sum_a + mirror(sum_b.astype(BF)).astype(F32)

    out_a = forward(idx, own, xa, gain_a, lgain_a)
    out_b = forward(idx, other, xb, gain_b, lgain_b)

    mats = total[:rank].reshape(2, rank // 2, 2, cols)
    mine = jnp.where(core == 0, mats[:, :, 0], mats[:, :, 1])
    yours = jnp.where(core == 0, mats[:, :, 1], mats[:, :, 0])
    got = dp_move(yours, fc=1)
    grads = jnp.where(
        core == 0, jnp.concatenate([mine, got], axis=1), jnp.concatenate([got, mine], axis=1)
    )
    row = total[rank].reshape(2, cols)
    grad_gain = jnp.where(core == 0, row[0], row[1])
    grad_lgain = lax.dynamic_slice(total[rank + 1, :rank], (place * (rank // NDP),), (rank // NDP,))
    return (
        out_a[None],
        out_b[None],
        back_a[None],
        back_b[None],
        grad_gain[None],
        grads[0].T[None],
        grad_lgain[None],
        grads[1][None],
    )


def solution(mesh):
    act = P("section", "dp", None)
    placed = (
        act,
        act,
        act,
        act,
        P(None, "section", "dp", None),
        P(None, "section", "dp", None),
        P("section", None),
        P("section", "dp", None),
        P("section", None),
        P("section", None, "dp"),
    )
    return jax.shard_map(
        body,
        mesh=mesh,
        in_specs=placed,
        out_specs=(act, act, act, act, P("section", "dp"), act, P("section", "dp"), P("section", None, "dp")),
        check_vma=False,
    )
```

```python
import functools

import jax
import jax.numpy as jnp
from jax import lax
from jax.experimental import pallas as pl
from jax.experimental.pallas import tpu as pltpu
from jax.sharding import PartitionSpec as P

EPS = 1e-06
LATE = 1
NX, NZ, NC = 4, 2, 2
NDP = NX * NZ * NC
CH = 1024
BF = jnp.bfloat16
F32 = jnp.float32


def dp_move(value, fx=0, fz=0, fc=0):
    pairs = []
    for i in range(NDP):
        x, z, c = i // 4, (i // 2) % 2, i % 2
        pairs.append((i, ((x + fx) % NX) * 4 + (z ^ fz) * 2 + (c ^ fc)))
    return lax.ppermute(value, "dp", pairs)


def mirror(value, fz=0):
    n = lax.axis_size("section")
    pairs = [
        (s * NDP + i, (n - 1 - s) * NDP + (i ^ (fz * NC))) for s in range(n) for i in range(NDP)
    ]
    return lax.ppermute(value, ("section", "dp"), pairs)


def relay(value, distance, fc=0):
    n = lax.axis_size("section")
    pairs = [
        ((s - distance) * NDP + i, s * NDP + (i ^ fc))
        for s in range(n)
        if 0 <= s - distance < n
        for i in range(NDP)
    ]
    return lax.ppermute(value, ("section", "dp"), pairs)


def after(value, *others):
    return lax.optimization_barrier((value, *others))[0]


def ring(near):
    return near, dp_move(near, fx=1), dp_move(near, fx=-1)


def far_halves(group):
    near, right, left = group
    return group + (dp_move(right[..., 0, :, :], fx=1), dp_move(left[..., 1, :, :], fx=-1))


def other_core(group):
    return tuple(dp_move(p, fc=1) for p in group)


def nt(a, b):
    return lax.dot_general(a, b, (((1,), (1,)), ((), ())), preferred_element_type=F32)


def nn(a, b):
    return lax.dot_general(a, b, (((1,), (0,)), ((), ())), preferred_element_type=F32)


def place_pieces(idx, pieces, wd, wu):
    x, z, c = idx[0], idx[1], idx[2]
    rows = wd.shape[0] // NDP

    def put(dst_ref, value, dx, dz, dc):
        place = ((x + dx) & 3) * 4 + ((z + dz) & 1) * 2 + ((c + dc) & 1)
        dst_ref[pl.ds(pl.multiple_of(place * rows, 64), rows), :] = value

    many = len(pieces) == 5 * NC
    for n in range(NZ * NC):
        dc, dz = n // NZ, n % NZ
        group = pieces[5 * dc : 5 * dc + 5] if many else pieces[5 * n : 5 * n + 5]
        at = (dz,) if many else ()
        for ref, dx in ((group[0], 0), (group[1], 3), (group[2], 1)):
            put(wd, ref[at + (0,)], dx, dz, dc)
            put(wu, ref[at + (1,)], dx, dz, dc)
        put(wd, group[3][at] if many else group[3][...], 2, dz, dc)
        put(wu, group[4][at] if many else group[4][...], 2, dz, dc)


def chunks(ref):
    return ref.shape[1] // CH


def ds(k):
    return pl.ds(pl.multiple_of(k * CH, CH), CH)


def norm_scale(x_ref):
    def step(k, acc):
        xf = x_ref[:, ds(k)].astype(F32)
        sq = xf * xf
        part = sq[:, :128]
        for j in range(1, CH // 128):
            part = part + sq[:, 128 * j : 128 * (j + 1)]
        return acc + part

    acc = lax.fori_loop(0, chunks(x_ref), step, jnp.zeros((x_ref.shape[0], 128), F32))
    return lax.rsqrt(jnp.sum(acc, axis=1, keepdims=True) / x_ref.shape[1] + EPS)


def latent_of(x_ref, gain_ref, wd, nrm_ref, scale):
    def step(k, acc):
        xf = x_ref[:, ds(k)].astype(F32)
        normed = (xf * scale * gain_ref[:, ds(k)]).astype(BF)
        if nrm_ref is not None:
            nrm_ref[:, ds(k)] = normed
        return acc + nn(normed, wd[ds(k), :])

    return lax.fori_loop(0, chunks(x_ref), step, jnp.zeros((x_ref.shape[0], wd.shape[1]), F32))


def forward_kernel(x_ref, gain_ref, lgain_ref, wd, wu, out_ref):
    scale = norm_scale(x_ref)
    latent = latent_of(x_ref, gain_ref, wd, None, scale)
    scale2 = lax.rsqrt(jnp.mean(latent * latent, axis=1, keepdims=True) + EPS)
    scaled = (latent * scale2 * lgain_ref[...]).astype(BF)

    def step(k, carry):
        y = x_ref[:, ds(k)].astype(F32) + nt(scaled, wu[ds(k), :])
        out_ref[:, ds(k)] = y.astype(BF)
        return carry

    lax.fori_loop(0, chunks(x_ref), step, 0)


def backward_core(x_ref, g_ref, gain_ref, lgain_ref, wd, wu, nrm_ref, dn_ref, dgain_ref, back_ref):
    scale = norm_scale(x_ref)
    latent = latent_of(x_ref, gain_ref, wd, nrm_ref, scale)
    scale2 = lax.rsqrt(jnp.mean(latent * latent, axis=1, keepdims=True) + EPS)
    n2 = latent * scale2
    lgain = lgain_ref[...]
    scaled = (n2 * lgain).astype(BF)

    def step_g(k, acc):
        return acc + nn(g_ref[:, ds(k)], wu[ds(k), :])

    rows = x_ref.shape[0]
    width = x_ref.shape[1]
    dsc = lax.fori_loop(0, chunks(x_ref), step_g, jnp.zeros((rows, wd.shape[1]), F32))
    dq = dsc.astype(BF).astype(F32)
    dlg = jnp.sum(dq * n2, axis=0, keepdims=True)
    dn2 = dq * lgain
    dlat = (scale2 * (dn2 - n2 * jnp.mean(dn2 * n2, axis=1, keepdims=True))).astype(BF)

    def step_n(k, acc):
        dn_bf = nt(dlat, wd[ds(k), :]).astype(BF)
        dn_ref[:, ds(k)] = dn_bf
        n1 = x_ref[:, ds(k)].astype(F32) * scale
        prod = dn_bf.astype(F32) * n1
        dgain_ref[:, ds(k)] = dgain_ref[:, ds(k)] + jnp.sum(prod, axis=0, keepdims=True)
        prod = prod * gain_ref[:, ds(k)]
        part = prod[:, :128]
        for j in range(1, CH // 128):
            part = part + prod[:, 128 * j : 128 * (j + 1)]
        return acc + part

    acc = lax.fori_loop(0, chunks(x_ref), step_n, jnp.zeros((rows, 128), F32))
    coeff = jnp.sum(acc, axis=1, keepdims=True) / width
    lean = scale * scale * coeff

    def step_x(k, carry):
        dx = dn_ref[:, ds(k)].astype(F32) * (gain_ref[:, ds(k)] * scale) - x_ref[:, ds(k)].astype(F32) * lean
        back_ref[:, ds(k)] = (g_ref[:, ds(k)].astype(F32) + dx).astype(BF)
        return carry

    lax.fori_loop(0, chunks(x_ref), step_x, 0)
    return scaled, dlat, dlg


def backward_first_kernel(idx, *refs):
    (x_ref, g_ref, gain_ref, lgain_ref, back_ref, nrm_ref, sc_ref, dlat_ref, dgain_ref, dlg_ref,
     wd, wu, dn_ref) = refs[-13:]
    place_pieces(idx, refs[:-13], wd, wu)
    dgain_ref[...] = jnp.zeros(dgain_ref.shape, F32)
    scaled, dlat, dlg = backward_core(
        x_ref, g_ref, gain_ref, lgain_ref, wd, wu, nrm_ref, dn_ref, dgain_ref, back_ref
    )
    sc_ref[...] = scaled
    dlat_ref[...] = dlat
    dlg_ref[...] = dlg


def backward_last_kernel(idx, x_ref, g_ref, gain_ref, lgain_ref, wd, wu, nrm0_ref, g0_ref, sc0_ref, dlat0_ref,
                         dgain0_ref, dlg0_ref, back_ref, *refs):
    keep, send, (dn_ref, nrm_ref, dgain_ref) = refs[:NX], refs[NX : 2 * NX], refs[2 * NX :]
    dgain_ref[...] = dgain0_ref[...]
    scaled, dlat, dlg = backward_core(
        x_ref, g_ref, gain_ref, lgain_ref, wd, wu, nrm_ref, dn_ref, dgain_ref, back_ref
    )
    rank = wd.shape[1]
    half = rank // 2
    span = x_ref.shape[1] // (NX * NZ)
    x, z, c = idx[0], idx[1], idx[2]

    def rows_of(first, second):
        whole = jnp.concatenate([first, second], axis=0).astype(F32).T
        low, high = whole[:half], whole[half:]
        return jnp.where(c == 0, whole, jnp.concatenate([high, low], axis=0)).astype(BF)

    dlat_t = rows_of(dlat0_ref[...], dlat)
    sc_t = rows_of(sc0_ref[...], scaled)
    dlg_all = jnp.concatenate([dlg0_ref[...] + dlg, jnp.zeros((1, span - rank), F32)], axis=1)
    spare = jnp.zeros((14, span), F32)
    for dx in (2, 1, 3, 0):
        for dz in range(NZ):
            lanes = pl.ds(pl.multiple_of((((x + dx) & 3) * NZ + ((z + dz) & 1)) * span, 128), span)
            n_all = jnp.concatenate([nrm0_ref[:, lanes], nrm_ref[:, lanes]], axis=0)
            g_all = jnp.concatenate([g0_ref[:, lanes], g_ref[:, lanes]], axis=0)
            for m, grad in ((0, nn(dlat_t, n_all).astype(BF)), (1, nn(sc_t, g_all).astype(BF))):
                keep[dx][dz, m * half : (m + 1) * half, :] = grad[:half]
                send[dx][dz, m * half : (m + 1) * half, :] = grad[half:]
            small = jnp.concatenate([dgain_ref[:, lanes], dlg_all, spare], axis=0).astype(BF)
            keep[dx][dz, rank : rank + 16, :] = small
            send[dx][dz, rank : rank + 16, :] = small


SMEM = functools.partial(pl.BlockSpec, memory_space=pltpu.SMEM)
VMEM = functools.partial(pl.BlockSpec, memory_space=pltpu.VMEM)


def forward(whole, x, gain, lgain, work=1):
    t, width = x.shape
    rank = lgain.shape[1]
    return pl.pallas_call(
        forward_kernel,
        out_shape=jax.ShapeDtypeStruct(x.shape, BF),
        in_specs=[VMEM()] * 5,
        out_specs=VMEM(),
        compiler_params=pltpu.CompilerParams(vmem_limit_bytes=6 << 20),
        cost_estimate=pl.CostEstimate(flops=4 * t * width * rank, transcendentals=0, bytes_accessed=4 * work * width * (t + rank)),
        name="forward",
    )(x, gain, lgain, *whole)


def backward_first(idx, pieces, x, g, gain, lgain):
    t, width = x.shape
    rank = lgain.shape[1]
    act = jax.ShapeDtypeStruct(x.shape, BF)
    lat = jax.ShapeDtypeStruct((t, rank), BF)
    mat = jax.ShapeDtypeStruct((width, rank), BF)
    return pl.pallas_call(
        backward_first_kernel,
        out_shape=(act, act, lat, lat, jax.ShapeDtypeStruct((1, width), F32), jax.ShapeDtypeStruct((1, rank), F32), mat, mat),
        in_specs=[SMEM()] + [VMEM()] * (len(pieces) + 4),
        out_specs=(VMEM(),) * 8,
        scratch_shapes=[pltpu.VMEM(x.shape, BF)],
        compiler_params=pltpu.CompilerParams(vmem_limit_bytes=8 << 20),
        cost_estimate=pl.CostEstimate(flops=6 * t * width * rank, transcendentals=0, bytes_accessed=4 * width * (2 * t + rank)),
        name="backward_first",
    )(idx, *pieces, x, g, gain, lgain)


def backward_last(idx, x, g, gain, lgain, first, g0):
    t, width = x.shape
    rank = lgain.shape[1]
    act = jax.ShapeDtypeStruct(x.shape, BF)
    span = width // (NX * NZ)
    block = jax.ShapeDtypeStruct((NZ, rank + 16, span), BF)
    _, nrm0, sc0, dlat0, dgain0, dlg0, wd, wu = first
    out = pl.pallas_call(
        backward_last_kernel,
        out_shape=(act,) + (block,) * (2 * NX),
        in_specs=[SMEM()] + [VMEM()] * 12,
        out_specs=(VMEM(),) * (1 + 2 * NX),
        scratch_shapes=[
            pltpu.VMEM(x.shape, BF),
            pltpu.VMEM(x.shape, BF),
            pltpu.VMEM((1, width), F32),
        ],
        compiler_params=pltpu.CompilerParams(vmem_limit_bytes=12 << 20),
        cost_estimate=pl.CostEstimate(flops=14 * t * width * rank, transcendentals=0, bytes_accessed=4 * width * (4 * t + 2 * rank)),
        name="backward_last",
    )(idx, x, g, gain, lgain, wd, wu, nrm0, g0, sc0, dlat0, dgain0, dlg0)
    return out[0], out[1 : 1 + NX], out[1 + NX :]


def pair_sums(keep, send, *others):
    half = (keep[0].shape[1] - 16) // 2
    recv = {dx: dp_move(send[dx], fc=1) for dx in (2, 1, 3, 0)}
    far = (keep[2].astype(F32) + recv[2].astype(F32)).astype(BF)
    far = after(far, *others)
    return dp_move(far[:, :half], fx=1), dp_move(far[:, half:], fx=-1), keep, recv


def ring_sums(parts):
    got_a, got_b, keep, recv = parts
    half = got_a.shape[1]
    rows = keep[0].shape[1]

    def both(dx):
        return keep[dx].astype(F32) + recv[dx].astype(F32)

    got_a = jnp.pad(got_a.astype(F32), ((0, 0), (0, rows - half), (0, 0)))
    got_b = jnp.pad(got_b.astype(F32), ((0, 0), (half, 0), (0, 0)))
    from_left = dp_move((both(1) + got_a).astype(BF), fx=1)
    from_right = dp_move((both(3) + got_b).astype(BF), fx=-1)
    return both(0) + from_left.astype(F32) + from_right.astype(F32)


def split_kernel(idx, own_ref, a_ref, b_ref, c_ref, mine_ref, yours_ref, row_ref, lrow_ref):
    total = own_ref[...] + a_ref[...].astype(F32) + b_ref[...].astype(F32) + c_ref[...].astype(F32)
    cols = yours_ref.shape[1]
    rows = yours_ref.shape[0]
    turned = pltpu.roll(total, cols, 1)
    first = idx[2] == 0
    mine = jnp.where(first, total, turned)
    mine_ref[...] = mine[:rows, : mine_ref.shape[1]]
    yours_ref[...] = jnp.where(first, turned, total)[:rows, :cols]
    row_ref[...] = mine[rows : rows + 1, :cols]
    lrow_ref[...] = total[rows + 1 : rows + 2, :rows]


def split_columns(idx, own, a, b, c, rank, cols):
    wide = -(-cols // 128) * 128
    return pl.pallas_call(
        split_kernel,
        out_shape=(
            jax.ShapeDtypeStruct((rank, wide), F32),
            jax.ShapeDtypeStruct((rank, cols), F32),
            jax.ShapeDtypeStruct((1, cols), F32),
            jax.ShapeDtypeStruct((1, rank), F32),
        ),
        in_specs=[SMEM()] + [VMEM()] * 4,
        out_specs=(VMEM(),) * 4,
        compiler_params=pltpu.CompilerParams(vmem_limit_bytes=16 << 20),
        name="split_columns",
    )(idx, own, a, b, c)


def join_kernel(idx, mine_ref, got_ref, down_ref, up_ref):
    rank, cols = got_ref.shape
    half = rank // 2
    first = idx[2] == 0
    wide = mine_ref.shape[1]
    got = jnp.concatenate([got_ref[...], jnp.zeros((rank, wide - cols), F32)], axis=1)
    mine = mine_ref[...]

    def whole(m):
        a, b = mine[m * half : (m + 1) * half], got[m * half : (m + 1) * half]
        return jnp.concatenate([jnp.where(first, a, b), jnp.where(first, b, a)], axis=0)

    down_ref[...] = whole(0).T[:cols]
    up_ref[...] = whole(1)[:, :cols]


def join_halves(idx, mine, got):
    rank, cols = got.shape
    return pl.pallas_call(
        join_kernel,
        out_shape=(jax.ShapeDtypeStruct((cols, rank), F32), jax.ShapeDtypeStruct((rank, cols), F32)),
        in_specs=[SMEM()] + [VMEM()] * 2,
        out_specs=(VMEM(),) * 2,
        compiler_params=pltpu.CompilerParams(vmem_limit_bytes=16 << 20),
        name="join_halves",
    )(idx, mine, got)


def body(enter_a, enter_b, cotan_a, cotan_b, saved_a, saved_b, norm_gain, w_down, latent_gain, w_up):
    place = lax.axis_index("dp")
    idx = (place.astype(jnp.int32) >> jnp.array([2, 1, 0], jnp.int32)) & jnp.array([3, 1, 1], jnp.int32)
    width = norm_gain.shape[1]
    rank = latent_gain.shape[1]
    cols = w_up.shape[2]

    shard = after(jnp.stack([w_down[0], w_up[0].T]), idx)
    across = dp_move(shard, fz=1)
    near_own = ring(shard)
    near_across = ring(after(across, near_own[1], near_own[2]))
    shard_m = after(shard, *near_across[1:])
    mirrored = mirror(shard_m)
    mirrored_z = mirror(shard_m, fz=1)
    near_own = far_halves(near_own)
    near_across = far_halves(near_across)
    pieces_a = near_own + near_across
    pieces_a = pieces_a + other_core(near_own) + other_core(near_across)
    gains = jnp.concatenate([norm_gain[0], latent_gain[0]]).reshape(-1, 128)
    gains_m = mirror(after(gains, *near_across[1:])).reshape(1, -1)
    gain_a, lgain_a = norm_gain, latent_gain
    gain_b, lgain_b = gains_m[:, :width], gains_m[:, width:]
    both_m = jnp.stack([mirrored, mirrored_z])
    near_m = ring(after(both_m, *near_own[3:], *near_across[3:]))

    first_a = backward_first(idx, pieces_a, saved_a[0, 0], cotan_a[0], gain_a, lgain_a)
    ga = relay(first_a[0], -1)
    near_m = far_halves(lax.optimization_barrier((*near_m, first_a[2]))[:3])
    pieces_b = near_m + other_core(near_m)
    first_b = backward_first(idx, pieces_b, saved_b[0, 0], cotan_b[0], gain_b, lgain_b)
    gb = relay(first_b[0], 1)
    ya = forward(first_a[6:], enter_a[0], gain_a, lgain_a)
    yb = forward(first_b[6:], enter_b[0], gain_b, lgain_b)
    xa = relay(ya, 1, fc=1)
    xb = relay(yb, -1, fc=1)

    back_a, keep_a, send_a = backward_last(idx, saved_a[1, 0], after(ga, ya, yb), gain_a, lgain_a, first_a, cotan_a[0])
    half_a = pair_sums(keep_a, send_a)
    gb = after(gb, ya, yb, half_a[0], half_a[1])
    back_b, keep_b, send_b = backward_last(idx, saved_b[1, 0], gb, gain_b, lgain_b, first_b, cotan_b[0])
    sums_a = ring_sums(half_a)
    sums_b = ring_sums(pair_sums(keep_b, send_b, sums_a))
    xa = dp_move(after(xa, sums_b), fc=1)
    xb = dp_move(after(xb, sums_b), fc=1)
    got_z = dp_move(sums_a[1].astype(BF), fz=1)
    got_m = mirror(sums_b[0].astype(BF))
    got_mz = mirror(sums_b[1].astype(BF), fz=1)
    mine, yours, row, lrow = split_columns(idx, sums_a[0], got_z, got_m, got_mz, rank, cols)
    out_a = forward(first_a[6:], xa, gain_a, lgain_a, LATE)
    out_b = forward(first_b[6:], xb, gain_b, lgain_b, LATE)
    yours, out_a, out_b = lax.optimization_barrier((yours, out_a, out_b))
    grad_down, grad_up = join_halves(idx, mine, dp_move(yours, fc=1))
    grad_lgain = lax.dynamic_slice(lrow, (jnp.uint32(0), place.astype(jnp.uint32) * (rank // NDP)), (1, rank // NDP))
    return (
        out_a[None],
        out_b[None],
        back_a[None],
        back_b[None],
        row,
        grad_down[None],
        grad_lgain,
        grad_up[None],
    )


def solution(mesh):
    act = P("section", "dp", None)
    placed = (
        act,
        act,
        act,
        act,
        P(None, "section", "dp", None),
        P(None, "section", "dp", None),
        P("section", None),
        P("section", "dp", None),
        P("section", None),
        P("section", None, "dp"),
    )
    return jax.shard_map(
        body,
        mesh=mesh,
        in_specs=placed,
        out_specs=(act, act, act, act, P("section", "dp"), act, P("section", "dp"), P("section", None, "dp")),
        check_vma=False,
    )
```

```python
import functools

import jax
import jax.numpy as jnp
from jax import lax
from jax.experimental import pallas as pl
from jax.experimental.pallas import tpu as pltpu
from jax.sharding import PartitionSpec as P

EPS = 1e-06
NX, NZ, NC = 4, 2, 2
NDP = NX * NZ * NC
CH = 1792
BF = jnp.bfloat16
F32 = jnp.float32


def dp_move(value, fx=0, fz=0, fc=0):
    pairs = []
    for i in range(NDP):
        x, z, c = i // 4, (i // 2) % 2, i % 2
        pairs.append((i, ((x + fx) % NX) * 4 + (z ^ fz) * 2 + (c ^ fc)))
    return lax.ppermute(value, "dp", pairs)


def mirror(value, fz=0):
    n = lax.axis_size("section")
    pairs = [
        (s * NDP + i, (n - 1 - s) * NDP + (i ^ (fz * NC))) for s in range(n) for i in range(NDP)
    ]
    return lax.ppermute(value, ("section", "dp"), pairs)


def relay(value, distance, fc=0):
    n = lax.axis_size("section")
    pairs = [
        ((s - distance) * NDP + i, s * NDP + (i ^ fc))
        for s in range(n)
        if 0 <= s - distance < n
        for i in range(NDP)
    ]
    return lax.ppermute(value, ("section", "dp"), pairs)


def halves(value):
    half = value.shape[0] // 2
    return value[:half], value[half:]


def after(value, *others):
    return lax.optimization_barrier((value, *others))[0]


def ring(near):
    return near, dp_move(near, fx=1), dp_move(near, fx=-1)


def far_halves(group):
    near, right, left = group
    return group + (dp_move(right[..., 0, :, :], fx=1), dp_move(left[..., 1, :, :], fx=-1))


def other_core(group):
    return tuple(dp_move(p, fc=1) for p in group)


def nt(a, b):
    return lax.dot_general(a, b, (((1,), (1,)), ((), ())), preferred_element_type=F32)


def nn(a, b):
    return lax.dot_general(a, b, (((1,), (0,)), ((), ())), preferred_element_type=F32)


def place_pieces(idx, pieces, wd, wu):
    x, z, c = idx[0], idx[1], idx[2]
    rows = wd.shape[0] // NDP

    def put(dst_ref, value, dx, dz, dc):
        place = ((x + dx) & 3) * 4 + ((z + dz) & 1) * 2 + ((c + dc) & 1)
        dst_ref[pl.ds(pl.multiple_of(place * rows, 64), rows), :] = value

    for n in range(NZ * NC):
        dc, dz = n // NZ, n % NZ
        near, right, left, far_a, far_b = pieces[5 * dc : 5 * dc + 5]
        for ref, dx in ((near, 0), (right, 3), (left, 1)):
            put(wd, ref[dz, 0], dx, dz, dc)
            put(wu, ref[dz, 1], dx, dz, dc)
        put(wd, far_a[dz], 2, dz, dc)
        put(wu, far_b[dz], 2, dz, dc)


def chunks(ref):
    return ref.shape[1] // CH


def ds(k):
    return pl.ds(pl.multiple_of(k * CH, CH), CH)


def norm_scale(x_ref):
    def step(k, acc):
        xf = x_ref[:, ds(k)].astype(F32)
        sq = xf * xf
        part = sq[:, :128]
        for j in range(1, CH // 128):
            part = part + sq[:, 128 * j : 128 * (j + 1)]
        return acc + part

    acc = lax.fori_loop(0, chunks(x_ref), step, jnp.zeros((x_ref.shape[0], 128), F32))
    return lax.rsqrt(jnp.sum(acc, axis=1, keepdims=True) / x_ref.shape[1] + EPS)


def latent_of(x_ref, gain_ref, wd, nrm_ref, scale):
    def step(k, acc):
        xf = x_ref[:, ds(k)].astype(F32)
        normed = (xf * scale * gain_ref[:, ds(k)]).astype(BF)
        if nrm_ref is not None:
            nrm_ref[:, ds(k)] = normed
        return acc + nn(normed, wd[ds(k), :])

    return lax.fori_loop(0, chunks(x_ref), step, jnp.zeros((x_ref.shape[0], wd.shape[1]), F32))


def forward_kernel(x_ref, gain_ref, lgain_ref, wd, wu, out_ref):
    count = out_ref.shape[0]
    x_ref = x_ref.at[x_ref.shape[0] - count :, :]
    scale = norm_scale(x_ref)
    latent = latent_of(x_ref, gain_ref, wd, None, scale)
    scale2 = lax.rsqrt(jnp.mean(latent * latent, axis=1, keepdims=True) + EPS)
    scaled = (latent * scale2 * lgain_ref[...]).astype(BF)

    def step(k, carry):
        y = x_ref[:, ds(k)].astype(F32) + nt(scaled, wu[ds(k), :])
        out_ref[:, ds(k)] = y.astype(BF)
        return carry

    lax.fori_loop(0, chunks(x_ref), step, 0)


def backward_core(x_ref, g_ref, gain_ref, lgain_ref, wd, wu, nrm_ref, dn_ref, dgain_ref, back_ref):
    scale = norm_scale(x_ref)
    latent = latent_of(x_ref, gain_ref, wd, nrm_ref, scale)
    scale2 = lax.rsqrt(jnp.mean(latent * latent, axis=1, keepdims=True) + EPS)
    n2 = latent * scale2
    lgain = lgain_ref[...]
    scaled = (n2 * lgain).astype(BF)

    def step_g(k, acc):
        return acc + nn(g_ref[:, ds(k)], wu[ds(k), :])

    rows = x_ref.shape[0]
    width = x_ref.shape[1]
    dsc = lax.fori_loop(0, chunks(x_ref), step_g, jnp.zeros((rows, wd.shape[1]), F32))
    dq = dsc.astype(BF).astype(F32)
    dlg = jnp.sum(dq * n2, axis=0, keepdims=True)
    dn2 = dq * lgain
    dlat = (scale2 * (dn2 - n2 * jnp.mean(dn2 * n2, axis=1, keepdims=True))).astype(BF)

    def step_n(k, acc):
        dn_bf = nt(dlat, wd[ds(k), :]).astype(BF)
        dn_ref[:, ds(k)] = dn_bf
        n1 = x_ref[:, ds(k)].astype(F32) * scale
        prod = dn_bf.astype(F32) * n1
        dgain_ref[:, ds(k)] = dgain_ref[:, ds(k)] + jnp.sum(prod, axis=0, keepdims=True)
        prod = prod * gain_ref[:, ds(k)]
        part = prod[:, :128]
        for j in range(1, CH // 128):
            part = part + prod[:, 128 * j : 128 * (j + 1)]
        return acc + part

    acc = lax.fori_loop(0, chunks(x_ref), step_n, jnp.zeros((rows, 128), F32))
    coeff = jnp.sum(acc, axis=1, keepdims=True) / width
    lean = scale * scale * coeff

    def step_x(k, carry):
        dx = dn_ref[:, ds(k)].astype(F32) * (gain_ref[:, ds(k)] * scale) - x_ref[:, ds(k)].astype(F32) * lean
        back_ref[:, ds(k)] = (g_ref[:, ds(k)].astype(F32) + dx).astype(BF)
        return carry

    lax.fori_loop(0, chunks(x_ref), step_x, 0)
    return scaled, dlat, dlg


def backward_first_kernel(idx, *refs):
    pieces, refs = refs[:10], refs[10:]
    if len(refs) > 13:
        rider_ref, refs = refs[0], refs[1:]
        count = rider_ref.shape[0]
        refs[4][count:, :] = rider_ref[...]
    (x_ref, g_ref, gain_ref, lgain_ref, back_ref, nrm_ref, sc_ref, dlat_ref, dgain_ref, dlg_ref,
     wd, wu, dn_ref) = refs
    place_pieces(idx, pieces, wd, wu)
    dgain_ref[...] = jnp.zeros(dgain_ref.shape, F32)
    scaled, dlat, dlg = backward_core(
        x_ref, g_ref, gain_ref, lgain_ref, wd, wu, nrm_ref, dn_ref, dgain_ref, back_ref.at[: x_ref.shape[0], :]
    )
    sc_ref[...] = scaled
    dlat_ref[...] = dlat
    dlg_ref[...] = dlg


def backward_last_kernel(idx, x_ref, g_ref, gain_ref, lgain_ref, wd, wu, nrm0_ref, g0_ref, sc0_ref, dlat0_ref,
                         dgain0_ref, dlg0_ref, back_ref, *refs):
    keep, send, (dn_ref, nrm_ref, dgain_ref) = refs[:NX], refs[NX : 2 * NX], refs[2 * NX :]
    dgain_ref[...] = dgain0_ref[...]
    g_ref = g_ref.at[: x_ref.shape[0], :]
    scaled, dlat, dlg = backward_core(
        x_ref, g_ref, gain_ref, lgain_ref, wd, wu, nrm_ref, dn_ref, dgain_ref, back_ref
    )
    rank = wd.shape[1]
    half = rank // 2
    span = x_ref.shape[1] // (NX * NZ)
    x, z, c = idx[0], idx[1], idx[2]

    def rows_of(first, second):
        whole = jnp.concatenate([first, second], axis=0).astype(F32).T
        low, high = whole[:half], whole[half:]
        return jnp.where(c == 0, whole, jnp.concatenate([high, low], axis=0)).astype(BF)

    dlat_t = rows_of(dlat0_ref[...], dlat)
    sc_t = rows_of(sc0_ref[...], scaled)
    dlg_all = jnp.concatenate([dlg0_ref[...] + dlg, jnp.zeros((1, span - rank), F32)], axis=1)
    spare = jnp.zeros((14, span), F32)
    for dx in (2, 1, 3, 0):
        for dz in range(NZ):
            lanes = pl.ds(pl.multiple_of((((x + dx) & 3) * NZ + ((z + dz) & 1)) * span, 128), span)
            n_all = jnp.concatenate([nrm0_ref[:, lanes], nrm_ref[:, lanes]], axis=0)
            g_all = jnp.concatenate([g0_ref[:, lanes], g_ref[:, lanes]], axis=0)
            for m, grad in ((0, nn(dlat_t, n_all).astype(BF)), (1, nn(sc_t, g_all).astype(BF))):
                keep[dx][dz, m * half : (m + 1) * half, :] = grad[:half]
                send[dx][dz, m * half : (m + 1) * half, :] = grad[half:]
            small = jnp.concatenate([dgain_ref[:, lanes], dlg_all, spare], axis=0).astype(BF)
            keep[dx][dz, rank : rank + 16, :] = small
            send[dx][dz, rank : rank + 16, :] = small


SMEM = functools.partial(pl.BlockSpec, memory_space=pltpu.SMEM)
VMEM = functools.partial(pl.BlockSpec, memory_space=pltpu.VMEM)


def forward(whole, x, gain, lgain, t):
    width = x.shape[1]
    rank = lgain.shape[1]
    return pl.pallas_call(
        forward_kernel,
        out_shape=jax.ShapeDtypeStruct((t, width), BF),
        in_specs=[VMEM()] * 5,
        out_specs=VMEM(),
        compiler_params=pltpu.CompilerParams(vmem_limit_bytes=6 << 20),
        cost_estimate=pl.CostEstimate(flops=t * width * rank, transcendentals=0, bytes_accessed=width * t),
        name="forward",
    )(x, gain, lgain, *whole)


def backward_first(idx, pieces, x, g, gain, lgain, rider=()):
    t, width = x.shape
    rank = lgain.shape[1]
    act = jax.ShapeDtypeStruct(x.shape, BF)
    lat = jax.ShapeDtypeStruct((t, rank), BF)
    mat = jax.ShapeDtypeStruct((width, rank), BF)
    return pl.pallas_call(
        backward_first_kernel,
        out_shape=(jax.ShapeDtypeStruct((t * (1 + len(rider)), width), BF), act, lat, lat, jax.ShapeDtypeStruct((1, width), F32), jax.ShapeDtypeStruct((1, rank), F32), mat, mat),
        in_specs=[SMEM()] + [VMEM()] * (len(pieces) + len(rider) + 4),
        out_specs=(VMEM(),) * 8,
        scratch_shapes=[pltpu.VMEM(x.shape, BF)],
        compiler_params=pltpu.CompilerParams(vmem_limit_bytes=8 << 20),
        cost_estimate=pl.CostEstimate(flops=6 * t * width * rank, transcendentals=0, bytes_accessed=4 * width * (2 * t + rank)),
        name="backward_first",
    )(idx, *pieces, *rider, x, g, gain, lgain)


def backward_last(idx, x, g, gain, lgain, first, g0):
    t, width = x.shape
    rank = lgain.shape[1]
    act = jax.ShapeDtypeStruct(x.shape, BF)
    span = width // (NX * NZ)
    block = jax.ShapeDtypeStruct((NZ, rank + 16, span), BF)
    _, nrm0, sc0, dlat0, dgain0, dlg0, wd, wu = first
    out = pl.pallas_call(
        backward_last_kernel,
        out_shape=(act,) + (block,) * (2 * NX),
        in_specs=[SMEM()] + [VMEM()] * 12,
        out_specs=(VMEM(),) * (1 + 2 * NX),
        scratch_shapes=[
            pltpu.VMEM(x.shape, BF),
            pltpu.VMEM(x.shape, BF),
            pltpu.VMEM((1, width), F32),
        ],
        compiler_params=pltpu.CompilerParams(vmem_limit_bytes=12 << 20),
        cost_estimate=pl.CostEstimate(flops=t * width * rank, transcendentals=0, bytes_accessed=width * t),
        name="backward_last",
    )(idx, x, g, gain, lgain, wd, wu, nrm0, g0, sc0, dlat0, dgain0, dlg0)
    return out[0], out[1 : 1 + NX], out[1 + NX :]


def pair_sums(keep, send, *others):
    half = (keep[0].shape[1] - 16) // 2
    recv = {dx: dp_move(send[dx], fc=1) for dx in (2, 1, 3, 0)}
    far = (keep[2].astype(F32) + recv[2].astype(F32)).astype(BF)
    far = after(far, *others)
    return dp_move(far[:, :half], fx=1), dp_move(far[:, half:], fx=-1), keep, recv


def ring_sums(parts, *others):
    got_a, got_b, keep, recv = parts
    half = got_a.shape[1]
    rows = keep[0].shape[1]

    def both(dx):
        return keep[dx].astype(F32) + recv[dx].astype(F32)

    got_a = jnp.pad(got_a.astype(F32), ((0, 0), (0, rows - half), (0, 0)))
    got_b = jnp.pad(got_b.astype(F32), ((0, 0), (half, 0), (0, 0)))
    to_right, to_left = lax.optimization_barrier(
        ((both(1) + got_a).astype(BF), (both(3) + got_b).astype(BF), *others)
    )[:2]
    from_left = dp_move(to_right, fx=1)
    from_right = dp_move(to_left, fx=-1)
    return both(0) + from_left.astype(F32) + from_right.astype(F32)


def direct_sums(keep, send):
    pairs = [k.astype(F32) + dp_move(b, fc=1).astype(F32) for k, b in zip(keep, send)]
    total = pairs[0]
    for dx in (2, 1, 3):
        total = total + dp_move(pairs[dx].astype(BF), fx=dx).astype(F32)
    return total


def split_kernel(idx, own_ref, a_ref, b_ref, c_ref, mine_ref, yours_ref, row_ref, lrow_ref):
    total = own_ref[...] + a_ref[...].astype(F32) + b_ref[...].astype(F32) + c_ref[...].astype(F32)
    cols = yours_ref.shape[1]
    rows = yours_ref.shape[0]
    turned = pltpu.roll(total, cols, 1)
    first = idx[2] == 0
    mine = jnp.where(first, total, turned)
    mine_ref[...] = mine[:rows, : mine_ref.shape[1]]
    yours_ref[...] = jnp.where(first, turned, total)[:rows, :cols]
    row_ref[...] = mine[rows : rows + 1, :cols]
    lrow_ref[...] = total[rows + 1 : rows + 2, :rows]


def split_columns(idx, own, a, b, c, rank, cols):
    wide = -(-cols // 128) * 128
    return pl.pallas_call(
        split_kernel,
        out_shape=(
            jax.ShapeDtypeStruct((rank, wide), F32),
            jax.ShapeDtypeStruct((rank, cols), F32),
            jax.ShapeDtypeStruct((1, cols), F32),
            jax.ShapeDtypeStruct((1, rank), F32),
        ),
        in_specs=[SMEM()] + [VMEM()] * 4,
        out_specs=(VMEM(),) * 4,
        compiler_params=pltpu.CompilerParams(vmem_limit_bytes=16 << 20),
        name="split_columns",
    )(idx, own, a, b, c)


def join_kernel(idx, mine_ref, got_ref, down_ref, up_ref):
    rank, cols = got_ref.shape
    half = rank // 2
    first = idx[2] == 0
    wide = mine_ref.shape[1]
    got = jnp.concatenate([got_ref[...], jnp.zeros((rank, wide - cols), F32)], axis=1)
    mine = mine_ref[...]

    def whole(m):
        a, b = mine[m * half : (m + 1) * half], got[m * half : (m + 1) * half]
        return jnp.concatenate([jnp.where(first, a, b), jnp.where(first, b, a)], axis=0)

    down_ref[...] = whole(0).T[:cols]
    up_ref[...] = whole(1)[:, :cols]


def join_halves(idx, mine, got):
    rank, cols = got.shape
    return pl.pallas_call(
        join_kernel,
        out_shape=(jax.ShapeDtypeStruct((cols, rank), F32), jax.ShapeDtypeStruct((rank, cols), F32)),
        in_specs=[SMEM()] + [VMEM()] * 2,
        out_specs=(VMEM(),) * 2,
        compiler_params=pltpu.CompilerParams(vmem_limit_bytes=16 << 20),
        name="join_halves",
    )(idx, mine, got)


def body(enter_a, enter_b, cotan_a, cotan_b, saved_a, saved_b, norm_gain, w_down, latent_gain, w_up):
    place = lax.axis_index("dp")
    idx = (place.astype(jnp.int32) >> jnp.array([2, 1, 0], jnp.int32)) & jnp.array([3, 1, 1], jnp.int32)
    width = norm_gain.shape[1]
    rank = latent_gain.shape[1]
    cols = w_up.shape[2]

    shard = after(jnp.stack([w_down[0], w_up[0].T]), idx)
    across = dp_move(shard, fz=1)
    near_own = ring(jnp.stack([shard, across]))
    shard_m = after(shard, across)
    mirrored = mirror(shard_m)
    mirrored_z = mirror(shard_m, fz=1)
    gains = jnp.concatenate([norm_gain[0], latent_gain[0]]).reshape(-1, 128)
    gains = mirror(after(gains, across))
    near_own = far_halves(lax.optimization_barrier((*near_own, gains))[:3])
    pieces_a = near_own + other_core(near_own)
    gains_m = gains.reshape(1, -1)
    gain_a, lgain_a = norm_gain, latent_gain
    gain_b, lgain_b = gains_m[:, :width], gains_m[:, width:]
    both_m = jnp.stack([mirrored, mirrored_z])
    near_m = ring(after(both_m, *near_own[3:]))

    first_a = backward_first(idx, pieces_a, saved_a[0, 0], cotan_a[0], gain_a, lgain_a)
    ga = [relay(h, -1) for h in halves(first_a[0])]
    near_m = far_halves(lax.optimization_barrier((*near_m, first_a[2]))[:3])
    pieces_b = near_m + other_core(near_m)
    t = enter_a.shape[1]
    ya = forward(first_a[6:], enter_a[0], gain_a, lgain_a, t)
    first_b = backward_first(
        idx, pieces_b, saved_b[0, 0], after(cotan_b[0], ga[0]), gain_b, lgain_b, [ya]
    )
    ahead = relay(first_b[0], 1)
    yb = forward(first_b[6:], after(enter_b[0], ga[1]), gain_b, lgain_b, t)

    ga = after(jnp.concatenate(ga), yb)
    back_a, keep_a, send_a = backward_last(idx, saved_a[1, 0], ga, gain_a, lgain_a, first_a, cotan_a[0])
    sums_a = direct_sums(keep_a, send_a)
    got_z = dp_move(sums_a[1].astype(BF), fz=1)
    ahead = after(ahead, sums_a)
    back_b, keep_b, send_b = backward_last(idx, saved_b[1, 0], ahead, gain_b, lgain_b, first_b, cotan_b[0])
    out_a = forward(first_a[6:], ahead, gain_a, lgain_a, t)
    sums_b = ring_sums(pair_sums(keep_b, send_b, sums_a), out_a)
    xb = dp_move(after(relay(after(yb, ahead, got_z), -1, fc=1), sums_b), fc=1)
    out_b = forward(first_b[6:], xb, gain_b, lgain_b, t)
    got_m = after(mirror(sums_b[0].astype(BF)), out_b)
    got_mz = mirror(sums_b[1].astype(BF), fz=1)
    mine, yours, row, lrow = split_columns(idx, sums_a[0], got_z, got_m, got_mz, rank, cols)
    yours = after(yours, out_b)
    grad_down, grad_up = join_halves(idx, mine, dp_move(yours, fc=1))
    grad_lgain = lax.dynamic_slice(lrow, (jnp.uint32(0), place.astype(jnp.uint32) * (rank // NDP)), (1, rank // NDP))
    return (
        out_a[None],
        out_b[None],
        back_a[None],
        back_b[None],
        row,
        grad_down[None],
        grad_lgain,
        grad_up[None],
    )


def solution(mesh):
    act = P("section", "dp", None)
    placed = (
        act,
        act,
        act,
        act,
        P(None, "section", "dp", None),
        P(None, "section", "dp", None),
        P("section", None),
        P("section", "dp", None),
        P("section", None),
        P("section", None, "dp"),
    )
    return jax.shard_map(
        body,
        mesh=mesh,
        in_specs=placed,
        out_specs=(act, act, act, act, P("section", "dp"), act, P("section", "dp"), P("section", None, "dp")),
        check_vma=False,
    )
```

```python
import functools

import jax
import jax.numpy as jnp
from jax import lax
from jax.experimental import pallas as pl
from jax.experimental.pallas import tpu as pltpu
from jax.sharding import PartitionSpec as P

EPS = 1e-06
NX, NZ, NC = 4, 2, 2
NDP = NX * NZ * NC
CH = 1792
BF = jnp.bfloat16
F32 = jnp.float32


def dp_move(value, fx=0, fz=0, fc=0):
    pairs = []
    for i in range(NDP):
        x, z, c = i // 4, (i // 2) % 2, i % 2
        pairs.append((i, ((x + fx) % NX) * 4 + (z ^ fz) * 2 + (c ^ fc)))
    return lax.ppermute(value, "dp", pairs)


def mirror(value, fz=0):
    n = lax.axis_size("section")
    pairs = [
        (s * NDP + i, (n - 1 - s) * NDP + (i ^ (fz * NC))) for s in range(n) for i in range(NDP)
    ]
    return lax.ppermute(value, ("section", "dp"), pairs)


def relay(value, distance, fc=0):
    n = lax.axis_size("section")
    pairs = [
        ((s - distance) * NDP + i, s * NDP + (i ^ fc))
        for s in range(n)
        if 0 <= s - distance < n
        for i in range(NDP)
    ]
    return lax.ppermute(value, ("section", "dp"), pairs)


def halves(value):
    half = value.shape[0] // 2
    return value[:half], value[half:]


def after(value, *others):
    return lax.optimization_barrier((value, *others))[0]


def ring(near):
    return near, dp_move(near, fx=1), dp_move(near, fx=-1)


def far_halves(group):
    near, right, left = group
    return group + (dp_move(right[..., 0, :, :], fx=1), dp_move(left[..., 1, :, :], fx=-1))


def other_core(group):
    return tuple(dp_move(p, fc=1) for p in group)


def nt(a, b):
    return lax.dot_general(a, b, (((1,), (1,)), ((), ())), preferred_element_type=F32)


def nn(a, b):
    return lax.dot_general(a, b, (((1,), (0,)), ((), ())), preferred_element_type=F32)


def place_pieces(idx, pieces, wd, wu):
    x, z, c = idx[0], idx[1], idx[2]
    rows = wd.shape[0] // NDP

    def put(dst_ref, value, dx, dz, dc):
        place = ((x + dx) & 3) * 4 + ((z + dz) & 1) * 2 + ((c + dc) & 1)
        dst_ref[pl.ds(pl.multiple_of(place * rows, 64), rows), :] = value

    for n in range(NZ * NC):
        dc, dz = n // NZ, n % NZ
        near, right, left, far_a, far_b = pieces[5 * dc : 5 * dc + 5]
        for ref, dx in ((near, 0), (right, 3), (left, 1)):
            put(wd, ref[dz, 0], dx, dz, dc)
            put(wu, ref[dz, 1], dx, dz, dc)
        put(wd, far_a[dz], 2, dz, dc)
        put(wu, far_b[dz], 2, dz, dc)


def chunks(ref):
    return ref.shape[1] // CH


def ds(k):
    return pl.ds(pl.multiple_of(k * CH, CH), CH)


def norm_scale(x_ref):
    def step(k, acc):
        xf = x_ref[:, ds(k)].astype(F32)
        sq = xf * xf
        part = sq[:, :128]
        for j in range(1, CH // 128):
            part = part + sq[:, 128 * j : 128 * (j + 1)]
        return acc + part

    acc = lax.fori_loop(0, chunks(x_ref), step, jnp.zeros((x_ref.shape[0], 128), F32))
    return lax.rsqrt(jnp.sum(acc, axis=1, keepdims=True) / x_ref.shape[1] + EPS)


def latent_of(x_ref, gain_ref, wd, nrm_ref, scale):
    def step(k, acc):
        xf = x_ref[:, ds(k)].astype(F32)
        normed = (xf * scale * gain_ref[:, ds(k)]).astype(BF)
        if nrm_ref is not None:
            nrm_ref[:, ds(k)] = normed
        return acc + nn(normed, wd[ds(k), :])

    return lax.fori_loop(0, chunks(x_ref), step, jnp.zeros((x_ref.shape[0], wd.shape[1]), F32))


def forward_kernel(x_ref, gain_ref, lgain_ref, wd, wu, out_ref):
    count = out_ref.shape[0]
    x_ref = x_ref.at[x_ref.shape[0] - count :, :]
    scale = norm_scale(x_ref)
    latent = latent_of(x_ref, gain_ref, wd, None, scale)
    scale2 = lax.rsqrt(jnp.mean(latent * latent, axis=1, keepdims=True) + EPS)
    scaled = (latent * scale2 * lgain_ref[...]).astype(BF)

    def step(k, carry):
        y = x_ref[:, ds(k)].astype(F32) + nt(scaled, wu[ds(k), :])
        out_ref[:, ds(k)] = y.astype(BF)
        return carry

    lax.fori_loop(0, chunks(x_ref), step, 0)


def backward_core(x_ref, g_ref, gain_ref, lgain_ref, wd, wu, nrm_ref, dn_ref, dgain_ref, back_ref):
    scale = norm_scale(x_ref)
    latent = latent_of(x_ref, gain_ref, wd, nrm_ref, scale)
    scale2 = lax.rsqrt(jnp.mean(latent * latent, axis=1, keepdims=True) + EPS)
    n2 = latent * scale2
    lgain = lgain_ref[...]
    scaled = (n2 * lgain).astype(BF)

    def step_g(k, acc):
        return acc + nn(g_ref[:, ds(k)], wu[ds(k), :])

    rows = x_ref.shape[0]
    width = x_ref.shape[1]
    dsc = lax.fori_loop(0, chunks(x_ref), step_g, jnp.zeros((rows, wd.shape[1]), F32))
    dq = dsc.astype(BF).astype(F32)
    dlg = jnp.sum(dq * n2, axis=0, keepdims=True)
    dn2 = dq * lgain
    dlat = (scale2 * (dn2 - n2 * jnp.mean(dn2 * n2, axis=1, keepdims=True))).astype(BF)

    def step_n(k, acc):
        dn_bf = nt(dlat, wd[ds(k), :]).astype(BF)
        dn_ref[:, ds(k)] = dn_bf
        n1 = x_ref[:, ds(k)].astype(F32) * scale
        prod = dn_bf.astype(F32) * n1
        dgain_ref[:, ds(k)] = dgain_ref[:, ds(k)] + jnp.sum(prod, axis=0, keepdims=True)
        prod = prod * gain_ref[:, ds(k)]
        part = prod[:, :128]
        for j in range(1, CH // 128):
            part = part + prod[:, 128 * j : 128 * (j + 1)]
        return acc + part

    acc = lax.fori_loop(0, chunks(x_ref), step_n, jnp.zeros((rows, 128), F32))
    coeff = jnp.sum(acc, axis=1, keepdims=True) / width
    lean = scale * scale * coeff

    def step_x(k, carry):
        dx = dn_ref[:, ds(k)].astype(F32) * (gain_ref[:, ds(k)] * scale) - x_ref[:, ds(k)].astype(F32) * lean
        back_ref[:, ds(k)] = (g_ref[:, ds(k)].astype(F32) + dx).astype(BF)
        return carry

    lax.fori_loop(0, chunks(x_ref), step_x, 0)
    return scaled, dlat, dlg


def backward_first_kernel(idx, *refs):
    pieces, refs = refs[:10], refs[10:]
    if len(refs) > 13:
        rider_ref, refs = refs[0], refs[1:]
        count = rider_ref.shape[0]
        refs[4][count:, :] = rider_ref[...]
    (x_ref, g_ref, gain_ref, lgain_ref, back_ref, nrm_ref, sc_ref, dlat_ref, dgain_ref, dlg_ref,
     wd, wu, dn_ref) = refs
    place_pieces(idx, pieces, wd, wu)
    dgain_ref[...] = jnp.zeros(dgain_ref.shape, F32)
    scaled, dlat, dlg = backward_core(
        x_ref, g_ref, gain_ref, lgain_ref, wd, wu, nrm_ref, dn_ref, dgain_ref, back_ref.at[: x_ref.shape[0], :]
    )
    sc_ref[...] = scaled
    dlat_ref[...] = dlat
    dlg_ref[...] = dlg


def backward_last_kernel(idx, x_ref, g_ref, gain_ref, lgain_ref, wd, wu, nrm0_ref, g0_ref, sc0_ref, dlat0_ref,
                         dgain0_ref, dlg0_ref, back_ref, *refs):
    keep, send, (dn_ref, nrm_ref, dgain_ref) = refs[:NX], refs[NX : 2 * NX], refs[2 * NX :]
    dgain_ref[...] = dgain0_ref[...]
    g_ref = g_ref.at[: x_ref.shape[0], :]
    scaled, dlat, dlg = backward_core(
        x_ref, g_ref, gain_ref, lgain_ref, wd, wu, nrm_ref, dn_ref, dgain_ref, back_ref
    )
    rank = wd.shape[1]
    half = rank // 2
    span = x_ref.shape[1] // (NX * NZ)
    x, z, c = idx[0], idx[1], idx[2]

    def rows_of(first, second):
        whole = jnp.concatenate([first, second], axis=0).astype(F32).T
        low, high = whole[:half], whole[half:]
        return jnp.where(c == 0, whole, jnp.concatenate([high, low], axis=0)).astype(BF)

    dlat_t = rows_of(dlat0_ref[...], dlat)
    sc_t = rows_of(sc0_ref[...], scaled)
    dlg_all = jnp.concatenate([dlg0_ref[...] + dlg, jnp.zeros((1, span - rank), F32)], axis=1)
    spare = jnp.zeros((14, span), F32)
    for dx in (2, 1, 3, 0):
        for dz in range(NZ):
            lanes = pl.ds(pl.multiple_of((((x + dx) & 3) * NZ + ((z + dz) & 1)) * span, 128), span)
            n_all = jnp.concatenate([nrm0_ref[:, lanes], nrm_ref[:, lanes]], axis=0)
            g_all = jnp.concatenate([g0_ref[:, lanes], g_ref[:, lanes]], axis=0)
            for m, grad in ((0, nn(dlat_t, n_all).astype(BF)), (1, nn(sc_t, g_all).astype(BF))):
                keep[dx][dz, m * half : (m + 1) * half, :] = grad[:half]
                send[dx][dz, m * half : (m + 1) * half, :] = grad[half:]
            small = jnp.concatenate([dgain_ref[:, lanes], dlg_all, spare], axis=0).astype(BF)
            keep[dx][dz, rank : rank + 16, :] = small
            send[dx][dz, rank : rank + 16, :] = small


SMEM = functools.partial(pl.BlockSpec, memory_space=pltpu.SMEM)
VMEM = functools.partial(pl.BlockSpec, memory_space=pltpu.VMEM)


def forward(whole, x, gain, lgain, t):
    width = x.shape[1]
    rank = lgain.shape[1]
    return pl.pallas_call(
        forward_kernel,
        out_shape=jax.ShapeDtypeStruct((t, width), BF),
        in_specs=[VMEM()] * 5,
        out_specs=VMEM(),
        compiler_params=pltpu.CompilerParams(vmem_limit_bytes=6 << 20),
        cost_estimate=pl.CostEstimate(flops=t * width * rank, transcendentals=0, bytes_accessed=width * t),
        name="forward",
    )(x, gain, lgain, *whole)


def backward_first(idx, pieces, x, g, gain, lgain, rider=()):
    t, width = x.shape
    rank = lgain.shape[1]
    act = jax.ShapeDtypeStruct(x.shape, BF)
    lat = jax.ShapeDtypeStruct((t, rank), BF)
    mat = jax.ShapeDtypeStruct((width, rank), BF)
    return pl.pallas_call(
        backward_first_kernel,
        out_shape=(jax.ShapeDtypeStruct((t * (1 + len(rider)), width), BF), act, lat, lat, jax.ShapeDtypeStruct((1, width), F32), jax.ShapeDtypeStruct((1, rank), F32), mat, mat),
        in_specs=[SMEM()] + [VMEM()] * (len(pieces) + len(rider) + 4),
        out_specs=(VMEM(),) * 8,
        scratch_shapes=[pltpu.VMEM(x.shape, BF)],
        compiler_params=pltpu.CompilerParams(vmem_limit_bytes=8 << 20),
        cost_estimate=pl.CostEstimate(flops=6 * t * width * rank, transcendentals=0, bytes_accessed=4 * width * (2 * t + rank)),
        name="backward_first",
    )(idx, *pieces, *rider, x, g, gain, lgain)


def backward_last(idx, x, g, gain, lgain, first, g0):
    t, width = x.shape
    rank = lgain.shape[1]
    act = jax.ShapeDtypeStruct(x.shape, BF)
    span = width // (NX * NZ)
    block = jax.ShapeDtypeStruct((NZ, rank + 16, span), BF)
    _, nrm0, sc0, dlat0, dgain0, dlg0, wd, wu = first
    out = pl.pallas_call(
        backward_last_kernel,
        out_shape=(act,) + (block,) * (2 * NX),
        in_specs=[SMEM()] + [VMEM()] * 12,
        out_specs=(VMEM(),) * (1 + 2 * NX),
        scratch_shapes=[
            pltpu.VMEM(x.shape, BF),
            pltpu.VMEM(x.shape, BF),
            pltpu.VMEM((1, width), F32),
        ],
        compiler_params=pltpu.CompilerParams(vmem_limit_bytes=12 << 20),
        cost_estimate=pl.CostEstimate(flops=t * width * rank, transcendentals=0, bytes_accessed=width * t),
        name="backward_last",
    )(idx, x, g, gain, lgain, wd, wu, nrm0, g0, sc0, dlat0, dgain0, dlg0)
    return out[0], out[1 : 1 + NX], out[1 + NX :]


def pair_sums(keep, send, *others):
    half = (keep[0].shape[1] - 16) // 2
    recv = {dx: dp_move(send[dx], fc=1) for dx in (2, 1, 3, 0)}
    far = (keep[2].astype(F32) + recv[2].astype(F32)).astype(BF)
    far = after(far, *others)
    return dp_move(far[:, :half], fx=1), dp_move(far[:, half:], fx=-1), keep, recv


def ring_sums(parts, *others):
    got_a, got_b, keep, recv = parts
    half = got_a.shape[1]
    rows = keep[0].shape[1]

    def both(dx):
        return keep[dx].astype(F32) + recv[dx].astype(F32)

    got_a = jnp.pad(got_a.astype(F32), ((0, 0), (0, rows - half), (0, 0)))
    got_b = jnp.pad(got_b.astype(F32), ((0, 0), (half, 0), (0, 0)))
    to_right, to_left = lax.optimization_barrier(
        ((both(1) + got_a).astype(BF), (both(3) + got_b).astype(BF), *others)
    )[:2]
    from_left = dp_move(to_right, fx=1)
    from_right = dp_move(to_left, fx=-1)
    return both(0) + from_left.astype(F32) + from_right.astype(F32)


def direct_sums(keep, send):
    pairs = [k.astype(F32) + dp_move(b, fc=1).astype(F32) for k, b in zip(keep, send)]
    total = pairs[0]
    for dx in (2, 1, 3):
        total = total + dp_move(pairs[dx].astype(BF), fx=dx).astype(F32)
    return total


def split_kernel(idx, own_ref, a_ref, b_ref, c_ref, mine_ref, yours_ref, row_ref, lrow_ref):
    total = own_ref[...] + a_ref[...].astype(F32) + b_ref[...].astype(F32) + c_ref[...].astype(F32)
    cols = yours_ref.shape[1]
    rows = yours_ref.shape[0]
    turned = pltpu.roll(total, cols, 1)
    first = idx[2] == 0
    mine = jnp.where(first, total, turned)
    mine_ref[...] = mine[:rows, : mine_ref.shape[1]]
    yours_ref[...] = jnp.where(first, turned, total)[:rows, :cols]
    row_ref[...] = mine[rows : rows + 1, :cols]
    lrow_ref[...] = total[rows + 1 : rows + 2, :rows]


def split_columns(idx, own, a, b, c, rank, cols):
    wide = -(-cols // 128) * 128
    return pl.pallas_call(
        split_kernel,
        out_shape=(
            jax.ShapeDtypeStruct((rank, wide), F32),
            jax.ShapeDtypeStruct((rank, cols), F32),
            jax.ShapeDtypeStruct((1, cols), F32),
            jax.ShapeDtypeStruct((1, rank), F32),
        ),
        in_specs=[SMEM()] + [VMEM()] * 4,
        out_specs=(VMEM(),) * 4,
        compiler_params=pltpu.CompilerParams(vmem_limit_bytes=16 << 20),
        name="split_columns",
    )(idx, own, a, b, c)


def join_kernel(idx, mine_ref, got_ref, down_ref, up_ref):
    rank, cols = got_ref.shape
    half = rank // 2
    first = idx[2] == 0
    wide = mine_ref.shape[1]
    got = jnp.concatenate([got_ref[...], jnp.zeros((rank, wide - cols), F32)], axis=1)
    mine = mine_ref[...]

    def whole(m):
        a, b = mine[m * half : (m + 1) * half], got[m * half : (m + 1) * half]
        return jnp.concatenate([jnp.where(first, a, b), jnp.where(first, b, a)], axis=0)

    down_ref[...] = whole(0).T[:cols]
    up_ref[...] = whole(1).T[:cols]


def join_halves(idx, mine, got):
    rank, cols = got.shape
    return pl.pallas_call(
        join_kernel,
        out_shape=(jax.ShapeDtypeStruct((cols, rank), F32), jax.ShapeDtypeStruct((cols, rank), F32)),
        in_specs=[SMEM()] + [VMEM()] * 2,
        out_specs=(VMEM(),) * 2,
        compiler_params=pltpu.CompilerParams(vmem_limit_bytes=16 << 20),
        name="join_halves",
    )(idx, mine, got)


def body(enter_a, enter_b, cotan_a, cotan_b, saved_a, saved_b, norm_gain, w_down, latent_gain, w_up):
    place = lax.axis_index("dp")
    idx = (place.astype(jnp.int32) >> jnp.array([2, 1, 0], jnp.int32)) & jnp.array([3, 1, 1], jnp.int32)
    width = norm_gain.shape[1]
    rank = latent_gain.shape[1]
    cols = w_up.shape[2]

    shard = after(jnp.stack([w_down[0], w_up[0].T]), idx)
    across = dp_move(shard, fz=1)
    gains = mirror(jnp.concatenate([norm_gain[0], latent_gain[0]]).reshape(-1, 128))
    near = ring(shard)
    near_z = ring(after(across, *near[1:], gains))
    near_own = tuple(jnp.stack(pair) for pair in zip(near, near_z))
    shard_m = after(shard, across)
    mirrored = mirror(shard_m)
    mirrored_z = mirror(shard_m, fz=1)
    near_own = far_halves(near_own)
    pieces_a = near_own + other_core(near_own)
    gains_m = gains.reshape(1, -1)
    gain_a, lgain_a = norm_gain, latent_gain
    gain_b, lgain_b = gains_m[:, :width], gains_m[:, width:]
    both_m = jnp.stack([mirrored, mirrored_z])
    near_m = ring(after(both_m, *near_own[3:]))

    first_a = backward_first(idx, pieces_a, saved_a[0, 0], cotan_a[0], gain_a, lgain_a)
    ga = [relay(h, -1) for h in halves(first_a[0])]
    near_m = far_halves(lax.optimization_barrier((*near_m, first_a[2]))[:3])
    pieces_b = near_m + other_core(near_m)
    t = enter_a.shape[1]
    ya = forward(first_a[6:], enter_a[0], gain_a, lgain_a, t)
    first_b = backward_first(
        idx, pieces_b, saved_b[0, 0], after(cotan_b[0], ga[0]), gain_b, lgain_b, [ya]
    )
    ahead = relay(first_b[0], 1)
    yb = forward(first_b[6:], after(enter_b[0], ga[1]), gain_b, lgain_b, t)

    ga = after(jnp.concatenate(ga), yb)
    back_a, keep_a, send_a = backward_last(idx, saved_a[1, 0], ga, gain_a, lgain_a, first_a, cotan_a[0])
    sums_a = direct_sums(keep_a, send_a)
    got_z = dp_move(sums_a[1].astype(BF), fz=1)
    ahead = after(ahead, sums_a)
    back_b, keep_b, send_b = backward_last(idx, saved_b[1, 0], ahead, gain_b, lgain_b, first_b, cotan_b[0])
    out_a = forward(first_a[6:], ahead, gain_a, lgain_a, t)
    sums_b = ring_sums(pair_sums(keep_b, send_b, sums_a), out_a)
    xb = dp_move(after(relay(after(yb, ahead, got_z), -1, fc=1), sums_b), fc=1)
    out_b = forward(first_b[6:], xb, gain_b, lgain_b, t)
    got_m = after(mirror(sums_b[0].astype(BF)), out_b)
    got_mz = mirror(sums_b[1].astype(BF), fz=1)
    mine, yours, row, lrow = split_columns(idx, sums_a[0], got_z, got_m, got_mz, rank, cols)
    yours = after(yours, out_b)
    grad_down, grad_up = join_halves(idx, mine, dp_move(yours, fc=1))
    grad_lgain = lax.dynamic_slice(lrow, (jnp.uint32(0), place.astype(jnp.uint32) * (rank // NDP)), (1, rank // NDP))
    return (
        out_a[None],
        out_b[None],
        back_a[None],
        back_b[None],
        row,
        grad_down[None],
        grad_lgain,
        grad_up.T[None],
    )


def solution(mesh):
    act = P("section", "dp", None)
    placed = (
        act,
        act,
        act,
        act,
        P(None, "section", "dp", None),
        P(None, "section", "dp", None),
        P("section", None),
        P("section", "dp", None),
        P("section", None),
        P("section", None, "dp"),
    )
    return jax.shard_map(
        body,
        mesh=mesh,
        in_specs=placed,
        out_specs=(act, act, act, act, P("section", "dp"), act, P("section", "dp"), P("section", None, "dp")),
        check_vma=False,
    )
```
